32 devices in a mesh: src: 16 (over z, y, x), lev: 2 (over core).
Axes of the slice: x: 2, y: 2, z: 4, core: 2. Of those that a mesh axis runs over, the one named last changes fastest.
Arguments:
- field: bfloat16 [32768, 256], P('src', 'lev'), may hold values from -6 to 6
- grad_coef: float32 [2, 4, 32768], P(None, None, 'src'), may hold values from -6 to 6
- neighbours: int32 [32768, 4], P('src'), may hold values from 0 to 2175, as said below
- level_weight: float32 [8], replicated, may hold values from 0.2 to 2
- src_index: int32 [2048, 64], P('src'), may hold values from 0 to 2047
- tgt_index: int32 [2048, 32], P('src'), may hold values from 0 to 1023
- block_dest: int32 [2048, 1], P('src'), may hold values from 0 to 15; in each aligned block of 128 rows (0 to 127, 128 to 255, ...) at most 16 rows name the same one
- weights: bfloat16 [2048, 6144], P('src'), may hold values from -0.21875 to 0.21875
Outputs:
- remapped: bfloat16 [16384, 256], P('src', 'lev')
- column_total: float32 [32, 16384], P(None, 'src')
The draws below stay inside these ranges and needn't reach their ends.
Inputs may be any that keep to these rules, and one draw needn't show every extreme that they name: `neighbours`: position 64 + p is the device's own cell p; positions below 64 and from 2112 on are the last and first cells of the devices before and after along the closed curve; a neighbour lies at most 64 cells from the cell. `block_dest`: the 128 blocks of one index of src name one target index at most 16 times.
All inputs are finite; a program needn't handle non-finite values.
Results may differ from the reference program's by a relative error of at most 0.0049.
Values may be sent and summed in bfloat16 or wider, within the bound.
A program may use at most 128 MiB of HBM per device.

```python
import math
import jax
import jax.numpy as jnp
import numpy as np
from jax import lax

FIELDS = 32
LEVELS = 8
K = 4
HW = 64
SB = 64
TB = 32
S_DEV = 2048
T_DEV = 1024
B_DEV = 128
SOURCES = 32768
TARGETS = 16384
BLOCKS = 2048
CAP = 16
COLS = 256
N_SRC = 16


def draw_neighbours(key, part):
    offsets = jax.random.randint(key, (SOURCES, K), -HW, HW + 1)
    position = jnp.arange(SOURCES, dtype=jnp.int32) % S_DEV
    first_column = jnp.where(position == 0, -HW, offsets[:, 0])
    first_column = jnp.where(position == S_DEV - 1, HW, first_column)
    offsets = jnp.concatenate([first_column[:, None], offsets[:, 1:]], axis=1)
    return (position[:, None] + HW + offsets).astype(jnp.int32)


def set_ends(array, key, low, top_value):
    index_at = [jax.random.randint(jax.random.fold_in(key, axis), (), 0, length) for axis, length in enumerate(array.shape)]
    widest = array.shape.index(max(array.shape))
    neighbour = index_at[:widest] + [(index_at[widest] + 1) % array.shape[widest]] + index_at[widest + 1:]
    return array.at[tuple(index_at)].set(low).at[tuple(neighbour)].set(top_value)


def block_scale(stream_key, extent, pieces, least, top_value):
    level = 1.0
    for dim, parts in pieces:
        draws = jax.random.uniform(jax.random.fold_in(jax.random.fold_in(stream_key, 6), dim), (parts,), jnp.float32, least / len(pieces), top_value / len(pieces))
        level = level * jnp.repeat(jnp.exp(draws), extent[dim] // parts).reshape((-1,) + (1,) * (len(extent) - 1 - dim))
    return level


def routed_block(own_key, own, number, rows, amount, top, bound, skew):
    ranking = jax.random.permutation(own_key, amount)
    packed, common = shares(amount, rows * top, bound, skew, True), shares(amount, rows * top, bound, skew, False)
    places = jnp.arange(amount)

    def named(tallies, turn):
        used = int((tallies > 0).sum())
        fixed = max(1, used // 4)
        passed = fixed + (places - fixed + turn * (used - fixed)) % max(1, amount - fixed)
        return jnp.zeros((amount,), jnp.int32).at[ranking[jnp.where(places < fixed, places, passed)]].set(jnp.asarray(tallies, jnp.int32))

    tallies = jnp.where(number % 4 == 0, named(packed, number // 4), named(common, number - number // 4 - 1))
    mixed = jax.random.permutation(jax.random.fold_in(own, 3), amount)
    giver, taker = mixed[0:amount // 2 * 2:2], mixed[1:amount // 2 * 2:2]
    margin = jnp.minimum(tallies[giver] - 1, bound - tallies[taker]) // 2
    margin = jnp.where((giver == ranking[0]) | (taker == ranking[0]) | (tallies[taker] == 0), 0, jnp.maximum(margin, 0))
    passed = jax.random.randint(jax.random.fold_in(own, 4), (amount // 2,), 0, 1 << 20) % (margin + 1)
    tallies = tallies.at[giver].add(-passed).at[taker].add(passed)
    members = jnp.searchsorted(jnp.cumsum(tallies), jnp.arange(rows * top), side="right").astype(jnp.int32)
    table = members.reshape(top, rows).T
    table = table[jax.random.permutation(jax.random.fold_in(own, 1), rows)]
    turn = jax.random.randint(jax.random.fold_in(own, 2), (rows, 1), 0, top)
    return jnp.take_along_axis(table, (jnp.arange(top)[None, :] + turn) % top, axis=1)


def shares(number_of, total, limit, slope, full):
    weights = [(1 << 20) // math.isqrt(grade ** slope) + 1 for grade in range(1, number_of + 1)]
    largest = limit if full else min(limit, max(-(-total // number_of), total * weights[0] // sum(weights)))
    least = 1 if total - largest >= number_of - 1 else 0
    given, spare = [largest] + [least] * (number_of - 1), total - largest - least * (number_of - 1)
    while spare > 0:
        free = [i for i in range(1, number_of) if given[i] < largest] or [i for i in range(1, number_of) if given[i] < limit]
        mass, left = sum([weights[i] for i in free]), spare
        for i in free:
            addition = min(limit - given[i], max(1, left * weights[i] // mass), spare)
            given[i] = given[i] + addition
            spare = spare - addition
    return np.array(given)


def scatter_about(stream_key, shape, spread, limit, cuts=(), held_as=jnp.bfloat16):
    result = spread * jax.random.normal(stream_key, shape, jnp.float32)
    if cuts:
        result = result * block_scale(stream_key, shape, cuts, -0.22, 0.18)
    return jnp.clip(result, -limit, limit).astype(held_as)


def setup_inputs(seed: int = 0) -> dict:
    splits = jax.random.split(jax.random.key(seed), 9)
    field = scatter_about(splits[0], (SOURCES, COLS), 1.0, 6.0, ((0, 16), (1, 2)))
    grad_coef = scatter_about(splits[1], (2, K, SOURCES), 1.0, 6.0, ((2, 16),), jnp.float32)
    neighbours = draw_neighbours(jax.random.fold_in(splits[8], 71), 0)
    level_weight = jnp.clip(jnp.exp(jax.random.uniform(splits[3], (LEVELS,), jnp.float32, math.log(0.2), math.log(2.0))), 0.2, 2.0)
    src_index = set_ends(jax.random.randint(splits[4], (BLOCKS, SB), 0, S_DEV), jax.random.fold_in(splits[4], 1), 0, S_DEV - 1).astype(jnp.int32)
    tgt_index = set_ends(jax.random.randint(splits[5], (BLOCKS, TB), 0, T_DEV), jax.random.fold_in(splits[5], 1), 0, T_DEV - 1).astype(jnp.int32)
    block_dest_keys = jax.random.split(jax.random.fold_in(splits[6], 1), BLOCKS // B_DEV)
    block_dest_turns = jax.random.permutation(jax.random.fold_in(splits[6], 3), BLOCKS // B_DEV)
    block_dest = jax.vmap(lambda own, number: routed_block(jax.random.fold_in(splits[6], 2), own, number, B_DEV, N_SRC, 1, CAP, 2))(block_dest_keys, block_dest_turns).reshape((BLOCKS, 1))
    weights = scatter_about(splits[7], (BLOCKS, 3 * SB * TB), (12 * SB) ** -0.5, 0.21875, ((0, 16),))
    return {"field": field, "grad_coef": grad_coef, "neighbours": neighbours, "level_weight": level_weight, "src_index": src_index, "tgt_index": tgt_index, "block_dest": block_dest, "weights": weights}


def device_partial(extended, coefficients, neighbour_pos, source_cells, block_weights):
    own_values = extended[HW:HW + S_DEV]
    own_float = own_values.astype(jnp.float32)
    differ = extended[neighbour_pos].astype(jnp.float32) - own_float[:, None, :]
    grad_east = jnp.sum(coefficients[0].T[:, :, None] * differ, axis=1).astype(jnp.bfloat16)
    grad_north = jnp.sum(coefficients[1].T[:, :, None] * differ, axis=1).astype(jnp.bfloat16)
    recon = jnp.stack([own_values, grad_east, grad_north])
    picked = recon[:, source_cells]
    block_rows = jnp.transpose(picked, (1, 0, 2, 3)).reshape(source_cells.shape[0], 3 * SB, -1)
    shaped = block_weights.reshape(source_cells.shape[0], 3 * SB, TB)
    return jnp.einsum('bjt,bjc->btc', shaped.astype(jnp.float32), block_rows.astype(jnp.float32))


def reference(field, grad_coef, neighbours, level_weight, src_index, tgt_index, block_dest, weights):
    padded = jnp.concatenate([field[-HW:], field, field[:HW]], axis=0)
    coefficients = grad_coef.reshape(2, K, N_SRC, S_DEV).transpose(2, 0, 1, 3)
    neighbour_pos = neighbours.reshape(N_SRC, S_DEV, K)
    source_cells = src_index.reshape(N_SRC, B_DEV, SB)
    target_cells = ((block_dest[:, 0] * T_DEV)[:, None] + tgt_index).reshape(N_SRC, B_DEV * TB)
    block_weights = weights.reshape(N_SRC, B_DEV, 3 * SB * TB)

    def accumulate(total, inputs):
        device, coef_dev, nbr_dev, cells_dev, rows_dev, weights_dev = inputs
        extended = lax.dynamic_slice_in_dim(padded, device * S_DEV, S_DEV + 2 * HW, 0)
        partial_value = device_partial(extended, coef_dev, nbr_dev, cells_dev, weights_dev)
        return total.at[rows_dev].add(partial_value.reshape(-1, COLS)), None

    start = jnp.zeros((TARGETS, COLS), jnp.float32)
    devices = jnp.arange(N_SRC, dtype=jnp.int32)
    total, _ = lax.scan(accumulate, start, (devices, coefficients, neighbour_pos, source_cells, target_cells, block_weights))
    remapped = total.astype(jnp.bfloat16)
    column_total = jnp.einsum('tlf,l->ft', total.reshape(TARGETS, LEVELS, FIELDS), level_weight, precision=lax.Precision.HIGHEST)
    return remapped, column_total
```

```python
import functools

import jax
import jax.numpy as jnp
from jax import lax
from jax.experimental import pallas as pl
from jax.experimental.pallas import tpu as pltpu
from jax.sharding import PartitionSpec as P

FIELDS = 32
HW = 64
SB = 64
TB = 32
T_DEV = 1024
LANES = 128
SUB = 8
TILE = 128
GROUP = LANES // TB
CHUNKS = ((0.0, 1.0),)


def contract_first(a, b):
    return lax.dot_general(a, b, (((0,), (0,)), ((), ())), preferred_element_type=jnp.float32)


def partial_kernel(
    first, last, src_count,
    src_ref, dest_ref, low_ref, field_ref, high_ref, coef_ref, near_ref, tgt_ref, weight_ref,
    send_ref, cells_ref,
    ext, recon, picked, count, block_list, slot_list,
):
    cells, columns = field_ref.shape
    blocks = tgt_ref.shape[0]
    ranks = last - first
    window = TILE + 2 * HW

    send_ref[...] = jnp.zeros_like(send_ref)
    cells_ref[...] = jnp.zeros_like(cells_ref)

    ext[0:HW, :] = low_ref[...]
    ext[HW:HW + cells, :] = field_ref[...]
    ext[HW + cells:HW + cells + HW, :] = high_ref[...]

    @pl.loop(0, src_count)
    def _(d):
        count[d] = 0

    def place(b, used):
        d = dest_ref[b]
        rank = count[d]
        count[d] = rank + 1
        block_list[used] = b
        slot_list[used] = d * ranks + rank - first
        taken = jnp.logical_and(rank >= first, rank < last)
        return used + taken.astype(jnp.int32)

    used = lax.fori_loop(0, blocks, place, jnp.int32(0))

    @pl.when(used > 0)
    def _():
        block_list[used] = block_list[used - 1]
        slot_list[used] = slot_list[used - 1]

    @pl.loop(0, cells // TILE)
    def _(t):
        base = pl.multiple_of(t * TILE, TILE)
        near = near_ref[:, pl.ds(base, TILE)] - base
        coef = [coef_ref[g, :, pl.ds(base, TILE)] for g in range(2)]
        place_w = lax.broadcasted_iota(jnp.int32, (window, TILE), 0)
        own = place_w == lax.broadcasted_iota(jnp.int32, (window, TILE), 1) + HW
        hits = [place_w == near[k:k + 1, :] for k in range(near.shape[0])]
        held = ext[pl.ds(base, window), :]
        rows = pl.multiple_of(base * SUB, TILE * SUB)
        recon[pl.ds(rows, TILE, stride=SUB), :] = field_ref[pl.ds(base, TILE), :].astype(
            jnp.float32
        )
        for g in range(2):
            total = -jnp.sum(coef[g], axis=0, keepdims=True)
            mix = jnp.where(own, total, 0.0)
            for k, hit in enumerate(hits):
                mix = mix + jnp.where(hit, coef[g][k:k + 1, :], 0.0)
            high = mix.astype(jnp.bfloat16)
            rest = (mix - high.astype(jnp.float32)).astype(jnp.bfloat16)
            value = contract_first(high, held) + contract_first(rest, held)
            recon[pl.ds(rows + 1 + g, TILE, stride=SUB), :] = value

    def one(n, buffer):
        b = block_list[n]
        slot = slot_list[n]
        for j in range(SB):
            at = pl.multiple_of(src_ref[j, b] * SUB, SUB)
            buffer[j * SUB:(j + 1) * SUB, :] = recon[pl.ds(at, SUB), :]
        held = weight_ref[b]
        total = None
        for q in range(GROUP):
            parts = [
                buffer[pl.ds(q * SUB + c, SB // GROUP, stride=GROUP * SUB), :] for c in range(3)
            ]
            rows = jnp.concatenate(parts, axis=0).astype(jnp.bfloat16)
            product = contract_first(held[:, q * TB:(q + 1) * TB], rows)
            total = product if total is None else total + product
        send_ref[slot] = total.astype(jnp.bfloat16)
        cells_ref[pl.ds(slot, 1), :] = tgt_ref[pl.ds(b, 1), :]

    @pl.loop(0, (used + 1) // 2)
    def _(n):
        one(2 * n, picked.at[0])
        one(2 * n + 1, picked.at[1])


def partials(first, last, src_count, src_t, dest, low, field, high, coef, near_t, tgt, weight):
    cells, columns = field.shape
    blocks = tgt.shape[0]
    slots = src_count * (last - first)
    smem = pl.BlockSpec(memory_space=pltpu.SMEM)
    vmem = pl.BlockSpec(memory_space=pltpu.VMEM)
    return pl.pallas_call(
        functools.partial(partial_kernel, first, last, src_count),
        out_shape=(
            jax.ShapeDtypeStruct((slots, TB, columns), jnp.bfloat16),
            jax.ShapeDtypeStruct((slots, TB), jnp.int32),
        ),
        in_specs=[smem, smem] + [vmem] * 7,
        out_specs=(vmem, vmem),
        scratch_shapes=[
            pltpu.VMEM((cells + 2 * HW, columns), jnp.bfloat16),
            pltpu.VMEM((cells * SUB, columns), jnp.float32),
            pltpu.VMEM((2, SB * SUB, columns), jnp.float32),
            pltpu.SMEM((src_count,), jnp.int32),
            pltpu.SMEM((blocks + 1,), jnp.int32),
            pltpu.SMEM((blocks + 1,), jnp.int32),
        ],
        compiler_params=pltpu.CompilerParams(vmem_limit_bytes=40 << 20),
        cost_estimate=pl.CostEstimate(
            flops=8 * blocks * SB * 3 * TB * columns,
            bytes_accessed=60_000_000,
            transcendentals=0,
        ),
        name="partials",
    )(src_t, dest, low, field, high, coef, near_t, tgt, weight)


def combine_kernel(parts, level_count, step, level_ref, *refs):
    index_refs, value_refs = refs[:parts], refs[parts:2 * parts]
    remapped_ref, sum_ref, total = refs[2 * parts:]
    targets, columns = total.shape
    total[...] = jnp.zeros_like(total)
    for index_ref, value_ref in zip(index_refs, value_refs):
        lines = step // LANES

        @pl.loop(0, value_ref.shape[0] // step)
        def _(n, index_ref=index_ref, value_ref=value_ref):
            place = lax.broadcasted_iota(jnp.int32, (targets, LANES), 0)
            hits = [
                jnp.where(place == index_ref[pl.ds(n * lines + m, 1), :], 1.0, 0.0).astype(
                    jnp.bfloat16
                )
                for m in range(lines)
            ]
            value = value_ref[pl.ds(pl.multiple_of(n * step, step), step), :]
            total[...] += jnp.dot(
                jnp.concatenate(hits, axis=1), value, preferred_element_type=jnp.float32
            )

    result = total[...]
    remapped_ref[...] = result.astype(jnp.bfloat16)
    start = lax.axis_index("lev") * level_count
    which = lax.broadcasted_iota(jnp.int32, (FIELDS, columns), 1)
    line = lax.broadcasted_iota(jnp.int32, (FIELDS, columns), 0)
    mix = jnp.zeros((FIELDS, columns), jnp.float32)
    for l in range(level_count):
        mix = jnp.where(which == line + l * FIELDS, level_ref[start + l], mix)
    sum_ref[...] = lax.dot_general(
        mix,
        result,
        (((1,), (1,)), ((), ())),
        precision=lax.Precision.HIGHEST,
        preferred_element_type=jnp.float32,
    )


def combine(level_weight, indices, values, level_count):
    columns = values[0].shape[1]
    smem = pl.BlockSpec(memory_space=pltpu.SMEM)
    vmem = pl.BlockSpec(memory_space=pltpu.VMEM)
    parts = len(values)
    rows = values[0].shape[0]
    step = 512 if all(v.shape[0] % 512 == 0 for v in values) else LANES
    return pl.pallas_call(
        functools.partial(combine_kernel, parts, level_count, step),
        out_shape=(
            jax.ShapeDtypeStruct((T_DEV, columns), jnp.bfloat16),
            jax.ShapeDtypeStruct((FIELDS, T_DEV), jnp.float32),
        ),
        in_specs=[smem] + [vmem] * (2 * parts),
        out_specs=(vmem, vmem),
        scratch_shapes=[pltpu.VMEM((T_DEV, columns), jnp.float32)],
        compiler_params=pltpu.CompilerParams(vmem_limit_bytes=40 << 20),
        name="combine",
    )(level_weight, *indices, *values)


def shards(field, grad_coef, neighbours, level_weight, src_index, tgt_index, block_dest, weights):
    src_count = lax.axis_size("src")
    forward = [(i, (i + 1) % src_count) for i in range(src_count)]
    backward = [(target, source) for source, target in forward]
    low = lax.ppermute(field[-HW:], "src", forward)
    high = lax.ppermute(field[:HW], "src", backward)
    columns = field.shape[1]
    blocks = src_index.shape[0]
    capacity = 2 * blocks // src_count
    shaped = weights.reshape(blocks, 3 * SB * TB // LANES, LANES)
    indices, values = [], []
    for begin, end in CHUNKS:
        first, last = int(begin * capacity), int(end * capacity)
        sent, cells = partials(
            first, last, src_count, src_index.T, block_dest[:, 0], low, field, high, grad_coef,
            neighbours.T, tgt_index, shaped,
        )
        width = (last - first) * TB
        cells = lax.all_to_all(
            cells.reshape(src_count, width), "src", split_axis=0, concat_axis=0, tiled=True
        )
        received = lax.all_to_all(sent, "src", split_axis=0, concat_axis=0, tiled=True)
        indices.append(cells.reshape(src_count * width // LANES, LANES))
        values.append(received.reshape(src_count * width, columns))
    remapped, local_sum = combine(level_weight, indices, values, columns // FIELDS)
    lev_count = lax.axis_size("lev")
    column_total = local_sum
    moving = local_sum
    for _ in range(lev_count - 1):
        moving = lax.ppermute(
            moving, "lev", [(i, (i + 1) % lev_count) for i in range(lev_count)]
        )
        column_total = column_total + moving
    return (remapped, column_total)


def solution(mesh):
    placed = (
        P("src", "lev"),
        P(None, None, "src"),
        P("src", None),
        P(),
        P("src", None),
        P("src", None),
        P("src", None),
        P("src", None),
    )
    return jax.shard_map(
        shards,
        mesh=mesh,
        in_specs=placed,
        out_specs=(P("src", "lev"), P(None, "src")),
        check_vma=False,
    )
```

```python
import functools

import jax
import jax.numpy as jnp
from jax import lax
from jax.experimental import pallas as pl
from jax.experimental.pallas import tpu as pltpu
from jax.sharding import PartitionSpec as P

FIELDS = 32
HW = 64
SB = 64
TB = 32
T_DEV = 1024
LANES = 128
SUB = 8
TILE = 128
GROUP = LANES // TB
MESH = pl.DeviceIdType.MESH


def contract_first(a, b):
    return lax.dot_general(a, b, (((0,), (0,)), ((), ())), preferred_element_type=jnp.float32)


def partial_kernel(
    capacity, src_count,
    src_ref, dest_ref, low_ref, field_ref, high_ref, coef_ref, near_ref, tgt_ref, weight_ref,
    send_ref,
    ext, recon, picked, tags, count, home,
):
    cells, columns = field_ref.shape
    blocks = tgt_ref.shape[0]
    rows_each = capacity * TB
    lines = tags.shape[0] // src_count
    window = TILE + 2 * HW

    send_ref[...] = jnp.zeros_like(send_ref)
    tags[...] = jnp.zeros_like(tags)

    ext[0:HW, :] = low_ref[...]
    ext[HW:HW + cells, :] = field_ref[...]
    ext[HW + cells:HW + cells + HW, :] = high_ref[...]

    @pl.loop(0, src_count)
    def _(d):
        count[d] = 0

    lane_group = lax.broadcasted_iota(jnp.int32, (1, LANES), 1) // TB

    @pl.loop(0, blocks)
    def _(b):
        d = dest_ref[b]
        rank = count[d]
        count[d] = rank + 1
        home[b] = d * capacity + rank
        line = pl.ds(d * lines + rank // GROUP, 1)
        tags[line, :] = jnp.where(
            lane_group == rank % GROUP, tgt_ref[pl.ds(b, 1), :], tags[line, :]
        )

    @pl.loop(0, src_count)
    def _(d):
        cell = tags[pl.ds(pl.multiple_of(d * lines, SUB), lines), :]
        digits = jnp.concatenate([cell // 256, cell % 256], axis=0).astype(jnp.float32)
        send_ref[d, rows_each:, :] = digits.astype(jnp.bfloat16)

    @pl.loop(0, cells // TILE)
    def _(t):
        base = pl.multiple_of(t * TILE, TILE)
        near = near_ref[:, pl.ds(base, TILE)] - base
        coef = [coef_ref[g, :, pl.ds(base, TILE)] for g in range(2)]
        place_w = lax.broadcasted_iota(jnp.int32, (window, TILE), 0)
        own = place_w == lax.broadcasted_iota(jnp.int32, (window, TILE), 1) + HW
        hits = [place_w == near[k:k + 1, :] for k in range(near.shape[0])]
        held = ext[pl.ds(base, window), :]
        rows = pl.multiple_of(base * SUB, TILE * SUB)
        recon[pl.ds(rows, TILE, stride=SUB), :] = field_ref[pl.ds(base, TILE), :].astype(
            jnp.float32
        )
        for g in range(2):
            total = -jnp.sum(coef[g], axis=0, keepdims=True)
            mix = jnp.where(own, total, 0.0)
            for k, hit in enumerate(hits):
                mix = mix + jnp.where(hit, coef[g][k:k + 1, :], 0.0)
            high = mix.astype(jnp.bfloat16)
            rest = (mix - high.astype(jnp.float32)).astype(jnp.bfloat16)
            value = contract_first(high, held) + contract_first(rest, held)
            recon[pl.ds(rows + 1 + g, TILE, stride=SUB), :] = value

    def one(b, buffer):
        slot = home[b]
        for j in range(SB):
            at = pl.multiple_of(src_ref[j, b] * SUB, SUB)
            buffer[j * SUB:(j + 1) * SUB, :] = recon[pl.ds(at, SUB), :]
        held = weight_ref[b]
        total = None
        for q in range(GROUP):
            parts = [
                buffer[pl.ds(q * SUB + c, SB // GROUP, stride=GROUP * SUB), :] for c in range(3)
            ]
            rows = jnp.concatenate(parts, axis=0).astype(jnp.bfloat16)
            product = contract_first(held[:, q * TB:(q + 1) * TB], rows)
            total = product if total is None else total + product
        row = pl.multiple_of(slot % capacity * TB, TB)
        send_ref[slot // capacity, pl.ds(row, TB), :] = total.astype(jnp.bfloat16)

    @pl.loop(0, blocks // 2)
    def _(n):
        one(2 * n, picked.at[0])
        one(2 * n + 1, picked.at[1])


def partials(capacity, src_count, src_t, dest, low, field, high, coef, near_t, tgt, weight):
    cells, columns = field.shape
    blocks = tgt.shape[0]
    lines = -(-capacity // (GROUP * SUB)) * SUB
    smem = pl.BlockSpec(memory_space=pltpu.SMEM)
    vmem = pl.BlockSpec(memory_space=pltpu.VMEM)
    return pl.pallas_call(
        functools.partial(partial_kernel, capacity, src_count),
        out_shape=jax.ShapeDtypeStruct(
            (src_count, capacity * TB + 2 * lines, columns), jnp.bfloat16
        ),
        in_specs=[smem, smem] + [vmem] * 7,
        out_specs=vmem,
        scratch_shapes=[
            pltpu.VMEM((cells + 2 * HW, columns), jnp.bfloat16),
            pltpu.VMEM((cells * SUB, columns), jnp.float32),
            pltpu.VMEM((2, SB * SUB, columns), jnp.float32),
            pltpu.VMEM((src_count * lines, LANES), jnp.int32),
            pltpu.SMEM((src_count,), jnp.int32),
            pltpu.SMEM((blocks,), jnp.int32),
        ],
        compiler_params=pltpu.CompilerParams(vmem_limit_bytes=40 << 20),
        cost_estimate=pl.CostEstimate(
            flops=8 * blocks * SB * 3 * TB * columns,
            bytes_accessed=60_000_000,
            transcendentals=0,
        ),
        name="partials",
    )(src_t, dest, low, field, high, coef, near_t, tgt, weight)


def exchange_kernel(
    count, level_count, lev_count, rows, level_ref, send_ref,
    remapped_ref, sum_ref,
    far_in, near_in, total, dense_out, dense_in, local_sum, other_sum,
    out_sem, in_sem, dense_sem, sum_sem,
):
    half = count // 2
    me = lax.axis_index("src")
    lev = lax.axis_index("lev")
    group = (me // half) * half
    place = me - group
    mirror = lax.rem(me + half, count)
    partner = lax.rem(lev + 1, lev_count)
    targets, columns = total.shape
    step = min(LANES, rows)
    lines = rows // step

    def peer(t):
        return group + lax.rem(place + t, half)

    barrier = pltpu.get_barrier_semaphore()

    @pl.loop(1, half)
    def _(t):
        pl.semaphore_signal(barrier, inc=1, device_id=(peer(t), lev), device_id_type=MESH)

    pl.semaphore_signal(barrier, inc=1, device_id=(mirror, lev), device_id_type=MESH)
    pl.semaphore_signal(barrier, inc=1, device_id=(me, partner), device_id_type=MESH)
    pl.semaphore_wait(barrier, half + 1)

    def copy(kind, t):
        to = peer(t)
        owner = lax.rem(to + half, count) if kind == 0 else to
        return pltpu.make_async_remote_copy(
            src_ref=send_ref.at[owner], dst_ref=(far_in, near_in)[kind].at[t],
            send_sem=out_sem.at[kind, t], recv_sem=in_sem.at[kind, t],
            device_id=(to, lev), device_id_type=MESH,
        )

    for kind in range(2):

        @pl.loop(1, half)
        def _(t, kind=kind):
            copy(kind, t).start()

    def add(chunk):
        digits = chunk[rows:, :].astype(jnp.float32)
        lead = digits.shape[0] // 2
        cell = (digits[:lead] * 256.0 + digits[lead:]).astype(jnp.int32)
        where = lax.broadcasted_iota(jnp.int32, (targets, step), 0)
        hits = [
            jnp.where(where == cell[m:m + 1, :step], 1.0, 0.0).astype(jnp.bfloat16)
            for m in range(lines)
        ]
        hits = hits[0] if lines == 1 else jnp.concatenate(hits, axis=1)
        total[...] += jnp.dot(hits, chunk[:rows, :], preferred_element_type=jnp.float32)

    total[...] = jnp.zeros_like(total)
    add(send_ref[mirror])

    @pl.loop(1, half)
    def _(t):
        copy(0, t).wait_recv()
        add(far_in[t])

    dense_out[...] = total[...].astype(jnp.bfloat16)
    dense = pltpu.make_async_remote_copy(
        src_ref=dense_out, dst_ref=dense_in, send_sem=dense_sem.at[0], recv_sem=dense_sem.at[1],
        device_id=(mirror, lev), device_id_type=MESH,
    )
    dense.start()
    total[...] = jnp.zeros_like(total)
    add(send_ref[me])

    @pl.loop(1, half)
    def _(t):
        copy(1, t).wait_recv()
        add(near_in[t])

    dense.wait_recv()
    result = total[...] + dense_in[...].astype(jnp.float32)
    remapped_ref[...] = result.astype(jnp.bfloat16)
    start = lev * level_count
    which = lax.broadcasted_iota(jnp.int32, (FIELDS, columns), 1)
    line = lax.broadcasted_iota(jnp.int32, (FIELDS, columns), 0)
    mix = jnp.zeros((FIELDS, columns), jnp.float32)
    for l in range(level_count):
        mix = jnp.where(which == line + l * FIELDS, level_ref[start + l], mix)
    local_sum[...] = lax.dot_general(
        mix,
        result,
        (((1,), (1,)), ((), ())),
        precision=lax.Precision.HIGHEST,
        preferred_element_type=jnp.float32,
    )
    swap = pltpu.make_async_remote_copy(
        src_ref=local_sum, dst_ref=other_sum, send_sem=sum_sem.at[0], recv_sem=sum_sem.at[1],
        device_id=(me, partner), device_id_type=MESH,
    )
    swap.start()

    @pl.loop(1, half)
    def _(t):
        copy(0, t).wait_send()
        copy(1, t).wait_send()

    dense.wait_send()
    swap.wait()
    sum_ref[...] = local_sum[...] + other_sum[...]


def exchange(level_weight, sent, rows, count, lev_count, level_count):
    columns = sent.shape[2]
    half = count // 2
    smem = pl.BlockSpec(memory_space=pltpu.SMEM)
    vmem = pl.BlockSpec(memory_space=pltpu.VMEM)
    landing = pltpu.VMEM((half,) + sent.shape[1:], jnp.bfloat16)
    return pl.pallas_call(
        functools.partial(exchange_kernel, count, level_count, lev_count, rows),
        out_shape=(
            jax.ShapeDtypeStruct((T_DEV, columns), jnp.bfloat16),
            jax.ShapeDtypeStruct((FIELDS, T_DEV), jnp.float32),
        ),
        in_specs=[smem, vmem],
        out_specs=(vmem, vmem),
        scratch_shapes=[
            landing,
            landing,
            pltpu.VMEM((T_DEV, columns), jnp.float32),
            pltpu.VMEM((T_DEV, columns), jnp.bfloat16),
            pltpu.VMEM((T_DEV, columns), jnp.bfloat16),
            pltpu.VMEM((FIELDS, T_DEV), jnp.float32),
            pltpu.VMEM((FIELDS, T_DEV), jnp.float32),
            pltpu.SemaphoreType.DMA((2, half)),
            pltpu.SemaphoreType.DMA((2, half)),
            pltpu.SemaphoreType.DMA((2,)),
            pltpu.SemaphoreType.DMA((2,)),
        ],
        compiler_params=pltpu.CompilerParams(
            vmem_limit_bytes=40 << 20, collective_id=0, has_side_effects=True
        ),
        name="exchange",
    )(level_weight, sent)


def shards(field, grad_coef, neighbours, level_weight, src_index, tgt_index, block_dest, weights):
    src_count = lax.axis_size("src")
    forward = [(i, (i + 1) % src_count) for i in range(src_count)]
    backward = [(target, source) for source, target in forward]
    low = lax.ppermute(field[-HW:], "src", forward)
    high = lax.ppermute(field[:HW], "src", backward)
    columns = field.shape[1]
    blocks = src_index.shape[0]
    capacity = 2 * blocks // src_count
    shaped = weights.reshape(blocks, 3 * SB * TB // LANES, LANES)
    sent = partials(
        capacity, src_count, src_index.T, block_dest[:, 0], low, field, high, grad_coef,
        neighbours.T, jnp.tile(tgt_index, (1, GROUP)), shaped,
    )
    return exchange(
        level_weight, sent, capacity * TB, src_count, lax.axis_size("lev"), columns // FIELDS
    )


def solution(mesh):
    placed = (
        P("src", "lev"),
        P(None, None, "src"),
        P("src", None),
        P(),
        P("src", None),
        P("src", None),
        P("src", None),
        P("src", None),
    )
    return jax.shard_map(
        shards,
        mesh=mesh,
        in_specs=placed,
        out_specs=(P("src", "lev"), P(None, "src")),
        check_vma=False,
    )
```

```python
import functools

import jax
import jax.numpy as jnp
from jax import lax
from jax.experimental import pallas as pl
from jax.experimental.pallas import tpu as pltpu
from jax.sharding import PartitionSpec as P

FIELDS = 32
HW = 64
SB = 64
TB = 32
T_DEV = 1024
LANES = 128
SUB = 8
TILE = 128
GROUP = LANES // TB
PIECE = 32
SPAN = SB + SUB
MESH = pl.DeviceIdType.MESH


def contract_first(a, b):
    return lax.dot_general(a, b, (((0,), (0,)), ((), ())), preferred_element_type=jnp.float32)


def partial_kernel(
    capacity, src_count,
    src_ref, home_ref, low_ref, field_ref, high_ref, coef_ref, near_ref, tgt_ref, weight_ref,
    send_ref,
    ext, recon, picked, tags, mixes,
):
    cells, columns = field_ref.shape
    blocks = tgt_ref.shape[0]
    rows_each = capacity * TB
    lines = tags.shape[0] // src_count
    window = TILE + 2 * HW

    send_ref[...] = jnp.zeros_like(send_ref)
    tags[...] = jnp.zeros_like(tags)

    ext[0:HW, :] = low_ref[...]
    ext[HW:HW + cells, :] = field_ref[...]
    ext[HW + cells:HW + cells + HW, :] = high_ref[...]

    lane_group = lax.broadcasted_iota(jnp.int32, (1, LANES), 1) // TB

    @pl.loop(0, cells // TILE)
    def _(t):
        base = pl.multiple_of(t * TILE, TILE)
        near = near_ref[:, pl.ds(base, TILE)] - base
        coef = [coef_ref[g, :, pl.ds(base, TILE)] for g in range(2)]
        totals = [-jnp.sum(coef[g], axis=0, keepdims=True) for g in range(2)]
        held = ext[pl.ds(base, window), :]
        rows = pl.multiple_of(base * SUB, TILE * SUB)
        recon[pl.ds(rows, TILE, stride=SUB), :] = field_ref[pl.ds(base, TILE), :].astype(
            jnp.float32
        )
        for w in range(0, window, PIECE):
            here = lax.broadcasted_iota(jnp.int32, (PIECE, TILE), 0) + w
            own = here == lax.broadcasted_iota(jnp.int32, (PIECE, TILE), 1) + HW
            mixed = [jnp.where(own, totals[g], 0.0) for g in range(2)]
            for k in range(near.shape[0]):
                hit = here == near[k:k + 1, :]
                for g in range(2):
                    mixed[g] = mixed[g] + jnp.where(hit, coef[g][k:k + 1, :], 0.0)
            for g in range(2):
                high = mixed[g].astype(jnp.bfloat16)
                rest = (mixed[g] - high.astype(jnp.float32)).astype(jnp.bfloat16)
                mixes[w:w + PIECE, 2 * g * TILE:(2 * g + 1) * TILE] = high
                mixes[w:w + PIECE, (2 * g + 1) * TILE:(2 * g + 2) * TILE] = rest
        for g in range(2):
            value = contract_first(mixes[:, 2 * g * TILE:(2 * g + 1) * TILE], held)
            value = value + contract_first(mixes[:, (2 * g + 1) * TILE:(2 * g + 2) * TILE], held)
            recon[pl.ds(rows + 1 + g, TILE, stride=SUB), :] = value

    def one(b, buffer):
        slot = home_ref[b]
        for j in range(SB):
            at = pl.multiple_of(src_ref[b, j], SUB)
            to = (j % GROUP) * (SB // GROUP) + j // GROUP
            buffer[pl.ds(to, 3, stride=SPAN), :] = recon[pl.ds(at, SUB), :][0:3, :]
        held = weight_ref[b]
        total = None
        for q in range(GROUP):
            parts = [
                buffer[pl.ds(c * SPAN + q * (SB // GROUP), SB // GROUP), :] for c in range(3)
            ]
            rows = jnp.concatenate(parts, axis=0).astype(jnp.bfloat16)
            product = contract_first(held[:, q * TB:(q + 1) * TB], rows)
            total = product if total is None else total + product
        owner = slot // capacity
        rank = slot % capacity
        row = pl.multiple_of(rank * TB, TB)
        send_ref[owner, pl.ds(row, TB), :] = total.astype(jnp.bfloat16)
        line = pl.ds(owner * lines + rank // GROUP, 1)
        tags[line, :] = jnp.where(
            lane_group == rank % GROUP, tgt_ref[pl.ds(b, 1), :], tags[line, :]
        )

    @pl.loop(0, blocks // 2)
    def _(n):
        one(2 * n, picked.at[0])
        one(2 * n + 1, picked.at[1])

    @pl.loop(0, src_count)
    def _(d):
        cell = tags[pl.ds(pl.multiple_of(d * lines, SUB), lines), :]
        digits = jnp.concatenate([cell // 256, cell % 256], axis=0).astype(jnp.float32)
        send_ref[d, rows_each:, :] = digits.astype(jnp.bfloat16)


def partials(capacity, src_count, src_rows, home, low, field, high, coef, near_t, tgt, weight):
    cells, columns = field.shape
    blocks = tgt.shape[0]
    lines = -(-capacity // (GROUP * SUB)) * SUB
    smem = pl.BlockSpec(memory_space=pltpu.SMEM)
    vmem = pl.BlockSpec(memory_space=pltpu.VMEM)
    return pl.pallas_call(
        functools.partial(partial_kernel, capacity, src_count),
        out_shape=jax.ShapeDtypeStruct(
            (src_count, capacity * TB + 2 * lines, columns), jnp.bfloat16
        ),
        in_specs=[smem, smem] + [vmem] * 7,
        out_specs=vmem,
        scratch_shapes=[
            pltpu.VMEM((cells + 2 * HW, columns), jnp.bfloat16),
            pltpu.VMEM((cells * SUB, columns), jnp.float32),
            pltpu.VMEM((2, 3 * SPAN, columns), jnp.float32),
            pltpu.VMEM((src_count * lines, LANES), jnp.int32),
            pltpu.VMEM((TILE + 2 * HW, 4 * TILE), jnp.bfloat16),
        ],
        compiler_params=pltpu.CompilerParams(vmem_limit_bytes=40 << 20),
        cost_estimate=pl.CostEstimate(
            flops=8 * blocks * SB * 3 * TB * columns,
            bytes_accessed=60_000_000,
            transcendentals=0,
        ),
        name="partials",
    )(src_rows, home, low, field, high, coef, near_t, tgt, weight)


def exchange_kernel(
    count, level_count, lev_count, rows, level_ref, send_ref,
    remapped_ref, sum_ref,
    far_in, near_in, total, dense_out, dense_in, local_sum, other_sum,
    out_sem, in_sem, dense_sem, sum_sem,
):
    half = count // 2
    me = lax.axis_index("src")
    lev = lax.axis_index("lev")
    group = (me // half) * half
    place = me - group
    mirror = lax.rem(me + half, count)
    partner = lax.rem(lev + 1, lev_count)
    targets, columns = total.shape
    step = min(LANES, rows)
    lines = rows // step

    def peer(t):
        return group + lax.rem(place + t, half)

    barrier = pltpu.get_barrier_semaphore()

    @pl.loop(1, half)
    def _(t):
        pl.semaphore_signal(barrier, inc=1, device_id=(peer(t), lev), device_id_type=MESH)

    pl.semaphore_signal(barrier, inc=1, device_id=(mirror, lev), device_id_type=MESH)
    pl.semaphore_signal(barrier, inc=1, device_id=(me, partner), device_id_type=MESH)
    pl.semaphore_wait(barrier, half + 1)

    def copy(kind, t):
        to = peer(t)
        owner = lax.rem(to + half, count) if kind == 0 else to
        return pltpu.make_async_remote_copy(
            src_ref=send_ref.at[owner], dst_ref=(far_in, near_in)[kind].at[t],
            send_sem=out_sem.at[kind, t], recv_sem=in_sem.at[kind, t],
            device_id=(to, lev), device_id_type=MESH,
        )

    for kind in range(2):

        @pl.loop(1, half)
        def _(t, kind=kind):
            copy(kind, t).start()

    def add(chunk):
        digits = chunk[rows:, :].astype(jnp.float32)
        lead = digits.shape[0] // 2
        cell = (digits[:lead] * 256.0 + digits[lead:]).astype(jnp.int32)
        where = lax.broadcasted_iota(jnp.int32, (targets, step), 0)
        hits = [
            jnp.where(where == cell[m:m + 1, :step], 1.0, 0.0).astype(jnp.bfloat16)
            for m in range(lines)
        ]
        hits = hits[0] if lines == 1 else jnp.concatenate(hits, axis=1)
        total[...] += jnp.dot(hits, chunk[:rows, :], preferred_element_type=jnp.float32)

    total[...] = jnp.zeros_like(total)
    add(send_ref[mirror])

    @pl.loop(1, half)
    def _(t):
        copy(0, t).wait_recv()
        add(far_in[t])

    dense_out[...] = total[...].astype(jnp.bfloat16)
    dense = pltpu.make_async_remote_copy(
        src_ref=dense_out, dst_ref=dense_in, send_sem=dense_sem.at[0], recv_sem=dense_sem.at[1],
        device_id=(mirror, lev), device_id_type=MESH,
    )
    dense.start()
    total[...] = jnp.zeros_like(total)
    add(send_ref[me])

    @pl.loop(1, half)
    def _(t):
        copy(1, t).wait_recv()
        add(near_in[t])

    dense.wait_recv()
    result = total[...] + dense_in[...].astype(jnp.float32)
    remapped_ref[...] = result.astype(jnp.bfloat16)
    start = lev * level_count
    which = lax.broadcasted_iota(jnp.int32, (FIELDS, columns), 1)
    line = lax.broadcasted_iota(jnp.int32, (FIELDS, columns), 0)
    mix = jnp.zeros((FIELDS, columns), jnp.float32)
    for l in range(level_count):
        mix = jnp.where(which == line + l * FIELDS, level_ref[start + l], mix)
    local_sum[...] = lax.dot_general(
        mix,
        result,
        (((1,), (1,)), ((), ())),
        precision=lax.Precision.HIGHEST,
        preferred_element_type=jnp.float32,
    )
    swap = pltpu.make_async_remote_copy(
        src_ref=local_sum, dst_ref=other_sum, send_sem=sum_sem.at[0], recv_sem=sum_sem.at[1],
        device_id=(me, partner), device_id_type=MESH,
    )
    swap.start()

    @pl.loop(1, half)
    def _(t):
        copy(0, t).wait_send()
        copy(1, t).wait_send()

    dense.wait_send()
    swap.wait()
    sum_ref[...] = local_sum[...] + other_sum[...]


def exchange(level_weight, sent, rows, count, lev_count, level_count):
    columns = sent.shape[2]
    half = count // 2
    smem = pl.BlockSpec(memory_space=pltpu.SMEM)
    vmem = pl.BlockSpec(memory_space=pltpu.VMEM)
    landing = pltpu.VMEM((half,) + sent.shape[1:], jnp.bfloat16)
    return pl.pallas_call(
        functools.partial(exchange_kernel, count, level_count, lev_count, rows),
        out_shape=(
            jax.ShapeDtypeStruct((T_DEV, columns), jnp.bfloat16),
            jax.ShapeDtypeStruct((FIELDS, T_DEV), jnp.float32),
        ),
        in_specs=[smem, vmem],
        out_specs=(vmem, vmem),
        scratch_shapes=[
            landing,
            landing,
            pltpu.VMEM((T_DEV, columns), jnp.float32),
            pltpu.VMEM((T_DEV, columns), jnp.bfloat16),
            pltpu.VMEM((T_DEV, columns), jnp.bfloat16),
            pltpu.VMEM((FIELDS, T_DEV), jnp.float32),
            pltpu.VMEM((FIELDS, T_DEV), jnp.float32),
            pltpu.SemaphoreType.DMA((2, half)),
            pltpu.SemaphoreType.DMA((2, half)),
            pltpu.SemaphoreType.DMA((2,)),
            pltpu.SemaphoreType.DMA((2,)),
        ],
        compiler_params=pltpu.CompilerParams(
            vmem_limit_bytes=40 << 20, collective_id=0, has_side_effects=True
        ),
        name="exchange",
    )(level_weight, sent)


def shards(field, grad_coef, neighbours, level_weight, src_index, tgt_index, block_dest, weights):
    src_count = lax.axis_size("src")
    forward = [(i, (i + 1) % src_count) for i in range(src_count)]
    backward = [(target, source) for source, target in forward]
    low = lax.ppermute(field[-HW:], "src", forward)
    high = lax.ppermute(field[:HW], "src", backward)
    columns = field.shape[1]
    blocks = src_index.shape[0]
    capacity = 2 * blocks // src_count
    owner = block_dest[:, 0]
    order = jnp.arange(blocks, dtype=jnp.int32)
    earlier = (owner[:, None] == owner[None, :]) & (order[:, None] < order[None, :])
    home = owner * capacity + jnp.sum(earlier.astype(jnp.int32), axis=0)
    shaped = weights.reshape(blocks, 3 * SB * TB // LANES, LANES)
    sent = partials(
        capacity, src_count, src_index * SUB, home, low, field, high, grad_coef,
        neighbours.T, jnp.tile(tgt_index, (1, GROUP)), shaped,
    )
    return exchange(
        level_weight, sent, capacity * TB, src_count, lax.axis_size("lev"), columns // FIELDS
    )


def solution(mesh):
    placed = (
        P("src", "lev"),
        P(None, None, "src"),
        P("src", None),
        P(),
        P("src", None),
        P("src", None),
        P("src", None),
        P("src", None),
    )
    return jax.shard_map(
        shards,
        mesh=mesh,
        in_specs=placed,
        out_specs=(P("src", "lev"), P(None, "src")),
        check_vma=False,
    )
```

```python
import functools

import jax
import jax.numpy as jnp
from jax import lax
from jax.experimental import pallas as pl
from jax.experimental.pallas import tpu as pltpu
from jax.sharding import PartitionSpec as P

FIELDS = 32
HW = 64
SB = 64
TB = 32
T_DEV = 1024
LANES = 128
SUB = 8
TILE = 128
GROUP = LANES // TB
GROUP_BITS = GROUP.bit_length() - 1
PIECE = 32
UNROLL = 4
BATCH = 16
SPAN = SB + SUB
MESH = pl.DeviceIdType.MESH


def tag_lines(capacity):
    return -(-capacity // (GROUP * SUB)) * SUB


def contract_first(a, b):
    return lax.dot_general(a, b, (((0,), (0,)), ((), ())), preferred_element_type=jnp.float32)


def partial_kernel(
    capacity, src_count,
    src_ref, row_ref, tag_ref, low_ref, field_ref, high_ref, coef_ref, near_ref, tgt_ref, weight_ref,
    send_ref,
    ext, recon, picked, tags, mixes,
):
    cells, columns = field_ref.shape
    blocks = tgt_ref.shape[0]
    rows_each = capacity * TB
    lines = tags.shape[0] // src_count
    window = TILE + 2 * HW

    send_ref[...] = jnp.zeros_like(send_ref)
    tags[...] = jnp.zeros_like(tags)

    ext[0:HW, :] = low_ref[...]
    ext[HW:HW + cells, :] = field_ref[...]
    ext[HW + cells:HW + cells + HW, :] = high_ref[...]

    lane_group = lax.broadcasted_iota(jnp.int32, (1, LANES), 1) // TB

    @pl.loop(0, cells // TILE)
    def _(t):
        base = pl.multiple_of(t * TILE, TILE)
        near = near_ref[:, pl.ds(base, TILE)] - base
        coef = [coef_ref[g, :, pl.ds(base, TILE)] for g in range(2)]
        totals = [-jnp.sum(coef[g], axis=0, keepdims=True) for g in range(2)]
        held = ext[pl.ds(base, window), :]
        rows = pl.multiple_of(base * SUB, TILE * SUB)
        recon[pl.ds(rows, TILE, stride=SUB), :] = field_ref[pl.ds(base, TILE), :].astype(
            jnp.float32
        )
        for w in range(0, window, PIECE):
            here = lax.broadcasted_iota(jnp.int32, (PIECE, TILE), 0) + w
            own = here == lax.broadcasted_iota(jnp.int32, (PIECE, TILE), 1) + HW
            mixed = [jnp.where(own, totals[g], 0.0) for g in range(2)]
            for k in range(near.shape[0]):
                hit = here == near[k:k + 1, :]
                for g in range(2):
                    mixed[g] = mixed[g] + jnp.where(hit, coef[g][k:k + 1, :], 0.0)
            for g in range(2):
                high = mixed[g].astype(jnp.bfloat16)
                rest = (mixed[g] - high.astype(jnp.float32)).astype(jnp.bfloat16)
                mixes[w:w + PIECE, 2 * g * TILE:(2 * g + 1) * TILE] = high
                mixes[w:w + PIECE, (2 * g + 1) * TILE:(2 * g + 2) * TILE] = rest
        for g in range(2):
            value = contract_first(mixes[:, 2 * g * TILE:(2 * g + 1) * TILE], held)
            value = value + contract_first(mixes[:, (2 * g + 1) * TILE:(2 * g + 2) * TILE], held)
            recon[pl.ds(rows + 1 + g, TILE, stride=SUB), :] = value

    def one(b, buffer):
        index = src_ref.at[b]
        for begin in range(0, SB, BATCH):
            found = [
                recon[pl.ds(pl.multiple_of(index[begin + j], SUB), SUB), :] for j in range(BATCH)
            ]
            for j in range(BATCH):
                to = ((begin + j) % GROUP) * (SB // GROUP) + (begin + j) // GROUP
                buffer[pl.ds(to, 3, stride=SPAN), :] = found[j][0:3, :]
        held = weight_ref[b]
        total = None
        for q in range(GROUP):
            parts = [
                buffer[pl.ds(c * SPAN + q * (SB // GROUP), SB // GROUP), :] for c in range(3)
            ]
            rows = jnp.concatenate(parts, axis=0).astype(jnp.bfloat16)
            product = contract_first(held[:, q * TB:(q + 1) * TB], rows)
            total = product if total is None else total + product
        send_ref[pl.ds(pl.multiple_of(row_ref[b], TB // 2), TB), :] = total.astype(jnp.bfloat16)
        tag = tag_ref[b]
        line = pl.ds(lax.shift_right_logical(tag, GROUP_BITS), 1)
        tags[line, :] = jnp.where(
            lane_group == jnp.bitwise_and(tag, GROUP - 1), tgt_ref[pl.ds(b, 1), :], tags[line, :]
        )

    @pl.loop(0, blocks // UNROLL)
    def _(n):
        for m in range(UNROLL):
            one(UNROLL * n + m, picked.at[m])

    @pl.loop(0, src_count)
    def _(d):
        cell = tags[pl.ds(pl.multiple_of(d * lines, SUB), lines), :]
        digits = jnp.concatenate([cell // 256, cell % 256], axis=0).astype(jnp.float32)
        at = pl.multiple_of(d * (rows_each + 2 * lines) + rows_each, 2 * SUB)
        send_ref[pl.ds(at, 2 * lines), :] = digits.astype(jnp.bfloat16)


def partials(capacity, src_count, src_rows, home_row, home_tag, low, field, high, coef, near_t, tgt, weight):
    cells, columns = field.shape
    blocks = tgt.shape[0]
    lines = tag_lines(capacity)
    smem = pl.BlockSpec(memory_space=pltpu.SMEM)
    vmem = pl.BlockSpec(memory_space=pltpu.VMEM)
    return pl.pallas_call(
        functools.partial(partial_kernel, capacity, src_count),
        out_shape=jax.ShapeDtypeStruct(
            (src_count * (capacity * TB + 2 * lines), columns), jnp.bfloat16
        ),
        in_specs=[smem] * 3 + [vmem] * 7,
        out_specs=vmem,
        scratch_shapes=[
            pltpu.VMEM((cells + 2 * HW, columns), jnp.bfloat16),
            pltpu.VMEM((cells * SUB, columns), jnp.float32),
            pltpu.VMEM((UNROLL, 3 * SPAN, columns), jnp.float32),
            pltpu.VMEM((src_count * lines, LANES), jnp.int32),
            pltpu.VMEM((TILE + 2 * HW, 4 * TILE), jnp.bfloat16),
        ],
        compiler_params=pltpu.CompilerParams(vmem_limit_bytes=40 << 20),
        cost_estimate=pl.CostEstimate(
            flops=8 * blocks * SB * 3 * TB * columns,
            bytes_accessed=60_000_000,
            transcendentals=0,
        ),
        name="partials",
    )(src_rows, home_row, home_tag, low, field, high, coef, near_t, tgt, weight)


def exchange_kernel(
    count, level_count, lev_count, rows, level_ref, send_ref,
    remapped_ref, sum_ref,
    far_in, near_in, total, dense_out, dense_in, local_sum, other_sum,
    out_sem, in_sem, dense_sem, sum_sem,
):
    half = count // 2
    me = lax.axis_index("src")
    lev = lax.axis_index("lev")
    group = (me // half) * half
    place = me - group
    mirror = lax.rem(me + half, count)
    partner = lax.rem(lev + 1, lev_count)
    targets, columns = total.shape
    step = min(LANES, rows)
    lines = rows // step

    def peer(t):
        return group + lax.rem(place + t, half)

    barrier = pltpu.get_barrier_semaphore()

    @pl.loop(1, half)
    def _(t):
        pl.semaphore_signal(barrier, inc=1, device_id=(peer(t), lev), device_id_type=MESH)

    pl.semaphore_signal(barrier, inc=1, device_id=(mirror, lev), device_id_type=MESH)
    pl.semaphore_signal(barrier, inc=1, device_id=(me, partner), device_id_type=MESH)
    pl.semaphore_wait(barrier, half + 1)

    def copy(kind, t):
        to = peer(t)
        owner = lax.rem(to + half, count) if kind == 0 else to
        return pltpu.make_async_remote_copy(
            src_ref=send_ref.at[owner], dst_ref=(far_in, near_in)[kind].at[t],
            send_sem=out_sem.at[kind, t], recv_sem=in_sem.at[kind, t],
            device_id=(to, lev), device_id_type=MESH,
        )

    for kind in range(2):

        @pl.loop(1, half)
        def _(t, kind=kind):
            copy(kind, t).start()

    def add(chunk):
        digits = chunk[rows:, :].astype(jnp.float32)
        lead = digits.shape[0] // 2
        cell = (digits[:lead] * 256.0 + digits[lead:]).astype(jnp.int32)
        where = lax.broadcasted_iota(jnp.int32, (targets, step), 0)
        hits = [
            jnp.where(where == cell[m:m + 1, :step], 1.0, 0.0).astype(jnp.bfloat16)
            for m in range(lines)
        ]
        hits = hits[0] if lines == 1 else jnp.concatenate(hits, axis=1)
        total[...] += jnp.dot(hits, chunk[:rows, :], preferred_element_type=jnp.float32)

    total[...] = jnp.zeros_like(total)
    add(send_ref[mirror])

    @pl.loop(1, half)
    def _(t):
        copy(0, t).wait_recv()
        add(far_in[t])

    dense_out[...] = total[...].astype(jnp.bfloat16)
    dense = pltpu.make_async_remote_copy(
        src_ref=dense_out, dst_ref=dense_in, send_sem=dense_sem.at[0], recv_sem=dense_sem.at[1],
        device_id=(mirror, lev), device_id_type=MESH,
    )
    dense.start()
    total[...] = jnp.zeros_like(total)
    add(send_ref[me])

    @pl.loop(1, half)
    def _(t):
        copy(1, t).wait_recv()
        add(near_in[t])

    dense.wait_recv()
    result = total[...] + dense_in[...].astype(jnp.float32)
    remapped_ref[...] = result.astype(jnp.bfloat16)
    start = lev * level_count
    which = lax.broadcasted_iota(jnp.int32, (FIELDS, columns), 1)
    line = lax.broadcasted_iota(jnp.int32, (FIELDS, columns), 0)
    mix = jnp.zeros((FIELDS, columns), jnp.float32)
    for l in range(level_count):
        mix = jnp.where(which == line + l * FIELDS, level_ref[start + l], mix)
    local_sum[...] = lax.dot_general(
        mix,
        result,
        (((1,), (1,)), ((), ())),
        precision=lax.Precision.HIGHEST,
        preferred_element_type=jnp.float32,
    )
    swap = pltpu.make_async_remote_copy(
        src_ref=local_sum, dst_ref=other_sum, send_sem=sum_sem.at[0], recv_sem=sum_sem.at[1],
        device_id=(me, partner), device_id_type=MESH,
    )
    swap.start()

    @pl.loop(1, half)
    def _(t):
        copy(0, t).wait_send()
        copy(1, t).wait_send()

    dense.wait_send()
    swap.wait()
    sum_ref[...] = local_sum[...] + other_sum[...]


def exchange(level_weight, sent, rows, count, lev_count, level_count):
    columns = sent.shape[2]
    half = count // 2
    smem = pl.BlockSpec(memory_space=pltpu.SMEM)
    vmem = pl.BlockSpec(memory_space=pltpu.VMEM)
    landing = pltpu.VMEM((half,) + sent.shape[1:], jnp.bfloat16)
    return pl.pallas_call(
        functools.partial(exchange_kernel, count, level_count, lev_count, rows),
        out_shape=(
            jax.ShapeDtypeStruct((T_DEV, columns), jnp.bfloat16),
            jax.ShapeDtypeStruct((FIELDS, T_DEV), jnp.float32),
        ),
        in_specs=[smem, vmem],
        out_specs=(vmem, vmem),
        scratch_shapes=[
            landing,
            landing,
            pltpu.VMEM((T_DEV, columns), jnp.float32),
            pltpu.VMEM((T_DEV, columns), jnp.bfloat16),
            pltpu.VMEM((T_DEV, columns), jnp.bfloat16),
            pltpu.VMEM((FIELDS, T_DEV), jnp.float32),
            pltpu.VMEM((FIELDS, T_DEV), jnp.float32),
            pltpu.SemaphoreType.DMA((2, half)),
            pltpu.SemaphoreType.DMA((2, half)),
            pltpu.SemaphoreType.DMA((2,)),
            pltpu.SemaphoreType.DMA((2,)),
        ],
        compiler_params=pltpu.CompilerParams(
            vmem_limit_bytes=40 << 20, collective_id=0, has_side_effects=True
        ),
        name="exchange",
    )(level_weight, sent)


def shards(field, grad_coef, neighbours, level_weight, src_index, tgt_index, block_dest, weights):
    src_count = lax.axis_size("src")
    forward = [(i, (i + 1) % src_count) for i in range(src_count)]
    backward = [(target, source) for source, target in forward]
    low = lax.ppermute(field[-HW:], "src", forward)
    high = lax.ppermute(field[:HW], "src", backward)
    columns = field.shape[1]
    blocks = src_index.shape[0]
    capacity = 2 * blocks // src_count
    owner = block_dest[:, 0]
    order = jnp.arange(blocks, dtype=jnp.int32)
    earlier = (owner[:, None] == owner[None, :]) & (order[:, None] < order[None, :])
    rank = jnp.sum(earlier.astype(jnp.int32), axis=0)
    lines = tag_lines(capacity)
    home_row = owner * (capacity * TB + 2 * lines) + rank * TB
    home_tag = owner * (lines * GROUP) + rank
    shaped = weights.reshape(blocks, 3 * SB * TB // LANES, LANES)
    sent = partials(
        capacity, src_count, src_index * SUB, home_row, home_tag, low, field, high, grad_coef,
        neighbours.T, jnp.tile(tgt_index, (1, GROUP)), shaped,
    )
    return exchange(
        level_weight, sent.reshape(src_count, -1, columns), capacity * TB, src_count, lax.axis_size("lev"), columns // FIELDS
    )


def solution(mesh):
    placed = (
        P("src", "lev"),
        P(None, None, "src"),
        P("src", None),
        P(),
        P("src", None),
        P("src", None),
        P("src", None),
        P("src", None),
    )
    return jax.shard_map(
        shards,
        mesh=mesh,
        in_specs=placed,
        out_specs=(P("src", "lev"), P(None, "src")),
        check_vma=False,
    )
```

```python
import functools

import jax
import jax.numpy as jnp
from jax import lax
from jax.experimental import pallas as pl
from jax.experimental.pallas import tpu as pltpu
from jax.sharding import PartitionSpec as P

FIELDS = 32
HW = 64
SB = 64
TB = 32
T_DEV = 1024
LANES = 128
SUB = 8
TILE = 128
GROUP = LANES // TB
GROUP_BITS = GROUP.bit_length() - 1
PIECE = 32
UNROLL = 4
BATCH = 16
SPAN = SB + SUB
MESH = pl.DeviceIdType.MESH


def tag_lines(capacity):
    return -(-capacity // (GROUP * SUB)) * SUB


def contract_first(a, b):
    return lax.dot_general(a, b, (((0,), (0,)), ((), ())), preferred_element_type=jnp.float32)


def prepare_kernel(count, field_ref, coef_ref, near_ref, recon, ext, mixes, out_sem, in_sem):
    cells = field_ref.shape[0]
    window = TILE + 2 * HW
    tiles = cells // TILE
    me = lax.axis_index("src")
    lev = lax.axis_index("lev")
    right = lax.rem(me + 1, count)
    left = lax.rem(me + count - 1, count)
    barrier = pltpu.get_barrier_semaphore()
    for other in (left, right):
        pl.semaphore_signal(barrier, inc=1, device_id=(other, lev), device_id_type=MESH)
    ext[HW:HW + cells, :] = field_ref[...]

    def tile(t):
        base = pl.multiple_of(t * TILE, TILE)
        near = near_ref[:, pl.ds(base, TILE)] - base
        coef = [coef_ref[g, :, pl.ds(base, TILE)] for g in range(2)]
        totals = [-jnp.sum(coef[g], axis=0, keepdims=True) for g in range(2)]
        held = ext[pl.ds(base, window), :]
        rows = pl.multiple_of(base * SUB, TILE * SUB)
        recon[pl.ds(rows, TILE, stride=SUB), :] = field_ref[pl.ds(base, TILE), :].astype(
            jnp.float32
        )
        for w in range(0, window, PIECE):
            here = lax.broadcasted_iota(jnp.int32, (PIECE, TILE), 0) + w
            own = here == lax.broadcasted_iota(jnp.int32, (PIECE, TILE), 1) + HW
            mixed = [jnp.where(own, totals[g], 0.0) for g in range(2)]
            for k in range(near.shape[0]):
                hit = here == near[k:k + 1, :]
                for g in range(2):
                    mixed[g] = mixed[g] + jnp.where(hit, coef[g][k:k + 1, :], 0.0)
            for g in range(2):
                high = mixed[g].astype(jnp.bfloat16)
                rest = (mixed[g] - high.astype(jnp.float32)).astype(jnp.bfloat16)
                mixes[w:w + PIECE, 2 * g * TILE:(2 * g + 1) * TILE] = high
                mixes[w:w + PIECE, (2 * g + 1) * TILE:(2 * g + 2) * TILE] = rest
        for g in range(2):
            value = contract_first(mixes[:, 2 * g * TILE:(2 * g + 1) * TILE], held)
            value = value + contract_first(mixes[:, (2 * g + 1) * TILE:(2 * g + 2) * TILE], held)
            recon[pl.ds(rows + 1 + g, TILE, stride=SUB), :] = value

    @pl.loop(1, tiles // 2)
    def _(t):
        tile(t)

    pl.semaphore_wait(barrier, 2)
    low = pltpu.make_async_remote_copy(
        src_ref=field_ref.at[pl.ds(cells - HW, HW)], dst_ref=ext.at[pl.ds(0, HW)],
        send_sem=out_sem.at[0], recv_sem=in_sem.at[0],
        device_id=(right, lev), device_id_type=MESH,
    )
    high = pltpu.make_async_remote_copy(
        src_ref=field_ref.at[pl.ds(0, HW)], dst_ref=ext.at[pl.ds(HW + cells, HW)],
        send_sem=out_sem.at[1], recv_sem=in_sem.at[1],
        device_id=(left, lev), device_id_type=MESH,
    )
    low.start()
    high.start()

    @pl.loop(tiles // 2, tiles - 1)
    def _(t):
        tile(t)

    low.wait()
    high.wait()

    @pl.loop(0, 2)
    def _(e):
        tile(e * (tiles - 1))


def prepare(count, field, coef, near_t):
    cells, columns = field.shape
    vmem = pl.BlockSpec(memory_space=pltpu.VMEM)
    return pl.pallas_call(
        functools.partial(prepare_kernel, count),
        out_shape=jax.ShapeDtypeStruct((cells * SUB, columns), jnp.float32),
        in_specs=[vmem] * 3,
        out_specs=vmem,
        scratch_shapes=[
            pltpu.VMEM((cells + 2 * HW, columns), jnp.bfloat16),
            pltpu.VMEM((TILE + 2 * HW, 4 * TILE), jnp.bfloat16),
            pltpu.SemaphoreType.DMA((2,)),
            pltpu.SemaphoreType.DMA((2,)),
        ],
        compiler_params=pltpu.CompilerParams(
            vmem_limit_bytes=24 << 20, collective_id=1, has_side_effects=True
        ),
        name="prepare",
    )(field, coef, near_t)


def partial_kernel(
    capacity, src_count,
    src_ref, row_ref, tag_ref, recon, tgt_ref, weight_ref,
    send_ref,
    picked, tags,
):
    blocks = tgt_ref.shape[0]
    rows_each = capacity * TB
    lines = tags.shape[0] // src_count

    send_ref[...] = jnp.zeros_like(send_ref)
    tags[...] = jnp.zeros_like(tags)

    lane_group = lax.broadcasted_iota(jnp.int32, (1, LANES), 1) // TB

    def one(b, buffer):
        index = src_ref.at[b]
        for begin in range(0, SB, BATCH):
            found = [
                recon[pl.ds(pl.multiple_of(index[begin + j], SUB), SUB), :] for j in range(BATCH)
            ]
            for j in range(BATCH):
                to = ((begin + j) % GROUP) * (SB // GROUP) + (begin + j) // GROUP
                buffer[pl.ds(to, 3, stride=SPAN), :] = found[j][0:3, :]
        held = weight_ref[b]
        total = None
        for q in range(GROUP):
            parts = [
                buffer[pl.ds(c * SPAN + q * (SB // GROUP), SB // GROUP), :] for c in range(3)
            ]
            rows = jnp.concatenate(parts, axis=0).astype(jnp.bfloat16)
            product = contract_first(held[:, q * TB:(q + 1) * TB], rows)
            total = product if total is None else total + product
        send_ref[pl.ds(pl.multiple_of(row_ref[b], TB // 2), TB), :] = total.astype(jnp.bfloat16)
        tag = tag_ref[b]
        line = pl.ds(lax.shift_right_logical(tag, GROUP_BITS), 1)
        tags[line, :] = jnp.where(
            lane_group == jnp.bitwise_and(tag, GROUP - 1), tgt_ref[pl.ds(b, 1), :], tags[line, :]
        )

    @pl.loop(0, blocks // UNROLL)
    def _(n):
        for m in range(UNROLL):
            one(UNROLL * n + m, picked.at[m])

    @pl.loop(0, src_count)
    def _(d):
        cell = tags[pl.ds(pl.multiple_of(d * lines, SUB), lines), :]
        digits = jnp.concatenate([cell // 256, cell % 256], axis=0).astype(jnp.float32)
        at = pl.multiple_of(d * (rows_each + 2 * lines) + rows_each, 2 * SUB)
        send_ref[pl.ds(at, 2 * lines), :] = digits.astype(jnp.bfloat16)


def partials(capacity, src_count, src_rows, home_row, home_tag, recon, tgt, weight):
    columns = recon.shape[1]
    blocks = tgt.shape[0]
    lines = tag_lines(capacity)
    smem = pl.BlockSpec(memory_space=pltpu.SMEM)
    vmem = pl.BlockSpec(memory_space=pltpu.VMEM)
    return pl.pallas_call(
        functools.partial(partial_kernel, capacity, src_count),
        out_shape=jax.ShapeDtypeStruct(
            (src_count * (capacity * TB + 2 * lines), columns), jnp.bfloat16
        ),
        in_specs=[smem] * 3 + [vmem] * 3,
        out_specs=vmem,
        scratch_shapes=[
            pltpu.VMEM((UNROLL, 3 * SPAN, columns), jnp.float32),
            pltpu.VMEM((src_count * lines, LANES), jnp.int32),
        ],
        compiler_params=pltpu.CompilerParams(vmem_limit_bytes=24 << 20),
        cost_estimate=pl.CostEstimate(
            flops=8 * blocks * SB * 3 * TB * columns,
            bytes_accessed=60_000_000,
            transcendentals=0,
        ),
        name="partials",
    )(src_rows, home_row, home_tag, recon, tgt, weight)


def exchange_kernel(
    count, level_count, lev_count, rows, level_ref, send_ref,
    remapped_ref, sum_ref,
    far_in, near_in, total, dense_out, dense_in, local_sum, other_sum,
    out_sem, in_sem, dense_sem, sum_sem,
):
    half = count // 2
    me = lax.axis_index("src")
    lev = lax.axis_index("lev")
    group = (me // half) * half
    place = me - group
    mirror = lax.rem(me + half, count)
    partner = lax.rem(lev + 1, lev_count)
    targets, columns = total.shape
    step = min(LANES, rows)
    lines = rows // step

    def peer(t):
        return group + lax.rem(place + t, half)

    barrier = pltpu.get_barrier_semaphore()

    @pl.loop(1, half)
    def _(t):
        pl.semaphore_signal(barrier, inc=1, device_id=(peer(t), lev), device_id_type=MESH)

    pl.semaphore_signal(barrier, inc=1, device_id=(mirror, lev), device_id_type=MESH)
    pl.semaphore_signal(barrier, inc=1, device_id=(me, partner), device_id_type=MESH)
    pl.semaphore_wait(barrier, half + 1)

    def copy(kind, t):
        to = peer(t)
        owner = lax.rem(to + half, count) if kind == 0 else to
        return pltpu.make_async_remote_copy(
            src_ref=send_ref.at[owner], dst_ref=(far_in, near_in)[kind].at[t],
            send_sem=out_sem.at[kind, t], recv_sem=in_sem.at[kind, t],
            device_id=(to, lev), device_id_type=MESH,
        )

    for kind in range(2):

        @pl.loop(1, half)
        def _(t, kind=kind):
            copy(kind, t).start()

    def add(chunk):
        digits = chunk[rows:, :].astype(jnp.float32)
        lead = digits.shape[0] // 2
        cell = (digits[:lead] * 256.0 + digits[lead:]).astype(jnp.int32)
        where = lax.broadcasted_iota(jnp.int32, (targets, step), 0)
        hits = [
            jnp.where(where == cell[m:m + 1, :step], 1.0, 0.0).astype(jnp.bfloat16)
            for m in range(lines)
        ]
        hits = hits[0] if lines == 1 else jnp.concatenate(hits, axis=1)
        total[...] += jnp.dot(hits, chunk[:rows, :], preferred_element_type=jnp.float32)

    total[...] = jnp.zeros_like(total)
    add(send_ref[mirror])

    @pl.loop(1, half)
    def _(t):
        copy(0, t).wait_recv()
        add(far_in[t])

    dense_out[...] = total[...].astype(jnp.bfloat16)
    dense = pltpu.make_async_remote_copy(
        src_ref=dense_out, dst_ref=dense_in, send_sem=dense_sem.at[0], recv_sem=dense_sem.at[1],
        device_id=(mirror, lev), device_id_type=MESH,
    )
    dense.start()
    total[...] = jnp.zeros_like(total)
    add(send_ref[me])

    @pl.loop(1, half)
    def _(t):
        copy(1, t).wait_recv()
        add(near_in[t])

    dense.wait_recv()
    result = total[...] + dense_in[...].astype(jnp.float32)
    remapped_ref[...] = result.astype(jnp.bfloat16)
    start = lev * level_count
    which = lax.broadcasted_iota(jnp.int32, (FIELDS, columns), 1)
    line = lax.broadcasted_iota(jnp.int32, (FIELDS, columns), 0)
    mix = jnp.zeros((FIELDS, columns), jnp.float32)
    for l in range(level_count):
        mix = jnp.where(which == line + l * FIELDS, level_ref[start + l], mix)
    local_sum[...] = lax.dot_general(
        mix,
        result,
        (((1,), (1,)), ((), ())),
        precision=lax.Precision.HIGHEST,
        preferred_element_type=jnp.float32,
    )
    swap = pltpu.make_async_remote_copy(
        src_ref=local_sum, dst_ref=other_sum, send_sem=sum_sem.at[0], recv_sem=sum_sem.at[1],
        device_id=(me, partner), device_id_type=MESH,
    )
    swap.start()

    @pl.loop(1, half)
    def _(t):
        copy(0, t).wait_send()
        copy(1, t).wait_send()

    dense.wait_send()
    swap.wait()
    sum_ref[...] = local_sum[...] + other_sum[...]


def exchange(level_weight, sent, rows, count, lev_count, level_count):
    columns = sent.shape[2]
    half = count // 2
    smem = pl.BlockSpec(memory_space=pltpu.SMEM)
    vmem = pl.BlockSpec(memory_space=pltpu.VMEM)
    landing = pltpu.VMEM((half,) + sent.shape[1:], jnp.bfloat16)
    return pl.pallas_call(
        functools.partial(exchange_kernel, count, level_count, lev_count, rows),
        out_shape=(
            jax.ShapeDtypeStruct((T_DEV, columns), jnp.bfloat16),
            jax.ShapeDtypeStruct((FIELDS, T_DEV), jnp.float32),
        ),
        in_specs=[smem, vmem],
        out_specs=(vmem, vmem),
        scratch_shapes=[
            landing,
            landing,
            pltpu.VMEM((T_DEV, columns), jnp.float32),
            pltpu.VMEM((T_DEV, columns), jnp.bfloat16),
            pltpu.VMEM((T_DEV, columns), jnp.bfloat16),
            pltpu.VMEM((FIELDS, T_DEV), jnp.float32),
            pltpu.VMEM((FIELDS, T_DEV), jnp.float32),
            pltpu.SemaphoreType.DMA((2, half)),
            pltpu.SemaphoreType.DMA((2, half)),
            pltpu.SemaphoreType.DMA((2,)),
            pltpu.SemaphoreType.DMA((2,)),
        ],
        compiler_params=pltpu.CompilerParams(
            vmem_limit_bytes=40 << 20, collective_id=0, has_side_effects=True
        ),
        name="exchange",
    )(level_weight, sent)


def shards(field, grad_coef, neighbours, level_weight, src_index, tgt_index, block_dest, weights):
    src_count = lax.axis_size("src")
    columns = field.shape[1]
    blocks = src_index.shape[0]
    capacity = 2 * blocks // src_count
    owner = block_dest[:, 0]
    order = jnp.arange(blocks, dtype=jnp.int32)
    earlier = (owner[:, None] == owner[None, :]) & (order[:, None] < order[None, :])
    rank = jnp.sum(earlier.astype(jnp.int32), axis=0)
    lines = tag_lines(capacity)
    home_row = owner * (capacity * TB + 2 * lines) + rank * TB
    home_tag = owner * (lines * GROUP) + rank
    shaped = weights.reshape(blocks, 3 * SB * TB // LANES, LANES)
    sent = partials(
        capacity, src_count, src_index * SUB, home_row, home_tag,
        prepare(src_count, field, grad_coef, neighbours.T), jnp.tile(tgt_index, (1, GROUP)), shaped,
    )
    return exchange(
        level_weight, sent.reshape(src_count, -1, columns), capacity * TB, src_count, lax.axis_size("lev"), columns // FIELDS
    )


def solution(mesh):
    placed = (
        P("src", "lev"),
        P(None, None, "src"),
        P("src", None),
        P(),
        P("src", None),
        P("src", None),
        P("src", None),
        P("src", None),
    )
    return jax.shard_map(
        shards,
        mesh=mesh,
        in_specs=placed,
        out_specs=(P("src", "lev"), P(None, "src")),
        check_vma=False,
    )
```
